256 devices in a mesh: pair: 16 (over y, z_lo, core), virt: 16 (over x, z_hi).
Axes of the slice: x: 4, y: 4, z: 8 (z_hi: 4, z_lo: 2; z = z_hi * 2 + z_lo), core: 2. Of those that a mesh axis runs over, the one named last changes fastest.
Arguments:
- amplitudes: float32 [16384, 1024], P('pair', 'virt'), may hold values from -6 to 6
- integrals: float32 [16384, 1024], P('virt', 'pair'), may hold values from -0.54 to 0.54
- residual_in: float32 [16384, 16384], P('pair', 'virt'), may hold values from -6 to 6
- pair_irrep: int32 [16384], P('pair'), may hold values from 0 to 7
- ab_irrep: int32 [16384], P('virt'), may hold values from 0 to 7
- cd_irrep: int32 [1024], replicated, may hold values from 0 to 7, as said below
Outputs:
- residual: float32 [16384, 16384], P('pair', 'virt')
The draws below stay inside these ranges and needn't reach their ends.
Inputs may be any that keep to these rules, and one draw needn't show every extreme that they name: `pair_irrep`: irrep labels. `ab_irrep`: irrep labels. `cd_irrep`: in every aligned block of 8 consecutive cd of the window, each of the 8 irreps labels exactly one cd.
All inputs are finite; a program needn't handle non-finite values.
Results may differ from the reference program's by a relative error of at most 0.00005.
Values sent between devices are 32-bit elements; how exact they have to be, the bound alone decides.
No kernel may reach another device: no remote copies, remote signals or barrier semaphores. Data moves between devices by JAX's collectives and lax.ppermute only.
A program may use at most 64 MiB of HBM per device.

```python
import jax
import jax.numpy as jnp
from jax import lax

CD = 1024
PAIRS = 16384
AB = 16384


def draw_cd_irrep(key, part):
    blocks = CD // 8
    scores = jax.random.randint(key, (blocks, 8), 0, 1048576) * 8 + jnp.arange(8, dtype=jnp.int32)[None, :]
    order = jnp.argsort(scores, axis=1)
    return order.reshape(CD).astype(jnp.int32)


def plant(entries, rng, smallest, largest):
    shape = entries.shape
    spot = [jax.random.randint(jax.random.fold_in(rng, axis), (), 0, shape[axis]) for axis in range(len(shape))]
    entries = entries.at[tuple(spot)].set(smallest)
    longest = shape.index(max(shape))
    spot[longest] = (spot[longest] + 1) % shape[longest]
    return entries.at[tuple(spot)].set(largest)


def levels(own_key, shape, pieces, low, top_value):
    def one(position, parts):
        draws = jax.random.uniform(jax.random.fold_in(jax.random.fold_in(own_key, 6), position), (parts,), jnp.float32, low / len(pieces), top_value / len(pieces))
        return jnp.repeat(jnp.exp(draws), shape[position] // parts).reshape((-1,) + (1,) * (len(shape) - position - 1))

    level = one(*pieces[0])
    for cut in pieces[1:]:
        level = level * one(*cut)
    return level


def noise(own_key, extent, width, bound, pieces=(), kind=jnp.bfloat16):
    loudness = levels(own_key, extent, pieces, -0.22, 0.18) if pieces else 1.0
    array = jax.random.normal(own_key, extent, jnp.float32) * width * loudness
    return jnp.minimum(jnp.maximum(array, -bound), bound).astype(kind)


def setup_inputs(seed: int = 0) -> dict:
    streams_of = jax.random.split(jax.random.key(seed), 7)
    amplitudes = noise(streams_of[0], (PAIRS, CD), 1.0, 6.0, ((0, 16), (1, 16)), jnp.float32)
    integrals = noise(streams_of[1], (AB, CD), 0.09, 0.54, ((0, 16), (1, 16)), jnp.float32)
    residual_in = noise(streams_of[2], (PAIRS, AB), 1.0, 6.0, ((0, 16), (1, 16)), jnp.float32)
    pair_irrep = plant(jax.random.randint(streams_of[3], (PAIRS,), 0, 8), jax.random.fold_in(streams_of[3], 1), 0, 7).astype(jnp.int32)
    ab_irrep = plant(jax.random.randint(streams_of[4], (AB,), 0, 8), jax.random.fold_in(streams_of[4], 1), 0, 7).astype(jnp.int32)
    cd_irrep = draw_cd_irrep(jax.random.fold_in(streams_of[6], 71), 0)
    return {"amplitudes": amplitudes, "integrals": integrals, "residual_in": residual_in, "pair_irrep": pair_irrep, "ab_irrep": ab_irrep, "cd_irrep": cd_irrep}


def reference(amplitudes, integrals, residual_in, pair_irrep, ab_irrep, cd_irrep):
    masked_t = jnp.where(pair_irrep[:, None] == cd_irrep[None, :], amplitudes, jnp.float32(0.0))
    masked_v = jnp.where(ab_irrep[:, None] == cd_irrep[None, :], integrals, jnp.float32(0.0))
    ladder = lax.dot_general(masked_t, masked_v, (((1,), (1,)), ((), ())), precision=lax.Precision.HIGHEST, preferred_element_type=jnp.float32)
    return residual_in + ladder
```

```python
import jax
import jax.numpy as jnp
from jax import lax
from jax.experimental import pallas as pl
from jax.experimental.pallas import tpu as pltpu
from jax.sharding import PartitionSpec as P

BLOCK = 8
LANES = 128


def column(row):
    return jnp.transpose(jnp.broadcast_to(row, (LANES, LANES)))


def compact_kernel(t_ref, v_ref, pair_ref, ab_ref, cd_ref, ct_ref, cv_ref):
    def one(x_ref, irrep_ref, index, out_ref):
        held = x_ref.shape[0]
        per_row = LANES // held
        labels = column(cd_ref[pl.ds(index // per_row, 1), :])
        part = labels[:held]
        for step in range(1, per_row):
            part = jnp.where(index % per_row == step, labels[step * held : (step + 1) * held], part)
        for group in range(x_ref.shape[1] // LANES):
            lanes = slice(group * LANES, (group + 1) * LANES)
            kept = jnp.where(part == irrep_ref[group : group + 1, :], x_ref[:, lanes], 0.0)
            out_ref[:, lanes] = jnp.sum(kept.reshape(held // BLOCK, BLOCK, LANES), axis=1)

    one(t_ref, pair_ref, lax.axis_index("virt"), ct_ref)
    one(v_ref, ab_ref, lax.axis_index("pair"), cv_ref)


def split(x):
    high = x.astype(jnp.bfloat16)
    low = (x - high.astype(jnp.float32)).astype(jnp.bfloat16)
    return high, low


def ladder_kernel(t_order, v_order, *refs):
    t_refs = refs[: len(t_order)]
    v_refs = refs[len(t_order) : len(t_order) + len(v_order)]
    residual_ref, pair_ref, ab_ref, out_ref, t_rows, v_rows, t_split, v_split = refs[len(t_order) + len(v_order) :]
    step = pl.program_id(0)
    depth = t_rows.shape[0]

    @pl.when(step == 0)
    def _():
        apart = lax.axis_index("virt") ^ lax.axis_index("pair")
        for order, ref in zip(t_order, t_refs):
            for slot, k in enumerate(order):
                at = pl.multiple_of((apart ^ k) * BLOCK, BLOCK)
                t_rows[pl.ds(at, BLOCK), :] = ref[slot * BLOCK : (slot + 1) * BLOCK, :]
        for order, ref in zip(v_order, v_refs):
            for slot, k in enumerate(order):
                v_rows[k * BLOCK : (k + 1) * BLOCK, :] = ref[slot * BLOCK : (slot + 1) * BLOCK, :]
        high, low = split(v_rows[...])
        v_split[:depth, :] = high
        v_split[depth : 2 * depth, :] = low
        v_split[2 * depth :, :] = high
        for group in range(t_rows.shape[1] // LANES):
            rows = slice(group * LANES, (group + 1) * LANES)
            high, low = split(jnp.transpose(t_rows[:, rows]))
            t_split[rows, :depth] = high
            t_split[rows, depth : 2 * depth] = high
            t_split[rows, 2 * depth :] = low

    rows = out_ref.shape[0]
    products = jnp.dot(
        t_split[pl.ds(pl.multiple_of(step * rows, rows), rows), :], v_split[...], preferred_element_type=jnp.float32
    )
    labels = column(pair_ref[pl.ds(step, 1), :])
    for group in range(out_ref.shape[1] // LANES):
        lanes = slice(group * LANES, (group + 1) * LANES)
        same = labels == ab_ref[group : group + 1, :]
        out_ref[:, lanes] = residual_ref[:, lanes] + jnp.where(same, products[:, lanes], 0.0)


def pairs(k):
    return [(i, i ^ k) for i in range(16)]


def gather(x, axis, stages):
    held, order = x, [0]
    for stage in stages[:-1]:
        pieces = [held] + [lax.ppermute(held, axis, pairs(k)) for k in stage]
        order = [o ^ k for k in (0, *stage) for o in order]
        held = jnp.concatenate(pieces, 0)
    pieces = [held] + [lax.ppermute(held, axis, pairs(k)) for k in stages[-1]]
    return pieces, [tuple(o ^ k for o in order) for k in (0, *stages[-1])]


def shards(amplitudes, integrals, residual_in, pair_irrep, ab_irrep, cd_irrep):
    rows, columns = residual_in.shape
    held_t, held_v = amplitudes.shape[1], integrals.shape[1]
    pair_rows = pair_irrep.reshape(-1, LANES)
    ab_rows = ab_irrep.reshape(-1, LANES)
    own_t, own_v = pl.pallas_call(
        compact_kernel,
        out_shape=(
            jax.ShapeDtypeStruct((held_t // BLOCK, rows), jnp.float32),
            jax.ShapeDtypeStruct((held_v // BLOCK, columns), jnp.float32),
        ),
        name="compact",
    )(amplitudes.T, integrals.T, pair_rows, ab_rows, cd_irrep.reshape(-1, LANES))
    t_pieces, t_order = gather(own_t, "virt", ((1, 3, 2), (4, 12, 8)))
    v_pieces, v_order = gather(own_v, "pair", ((8, 4, 12), (2,), (1,)))
    depth = 16 * BLOCK
    tile = LANES
    whole = pl.BlockSpec(memory_space=pltpu.VMEM)
    return pl.pallas_call(
        lambda *refs: ladder_kernel(t_order, v_order, *refs),
        grid=(rows // tile,),
        in_specs=[whole] * (len(t_pieces) + len(v_pieces))
        + [pl.BlockSpec((tile, columns), lambda i: (i, 0)), whole, whole],
        out_specs=pl.BlockSpec((tile, columns), lambda i: (i, 0)),
        out_shape=jax.ShapeDtypeStruct((rows, columns), jnp.float32),
        scratch_shapes=[
            pltpu.VMEM((depth, rows), jnp.float32),
            pltpu.VMEM((depth, columns), jnp.float32),
            pltpu.VMEM((rows, 3 * depth), jnp.bfloat16),
            pltpu.VMEM((3 * depth, columns), jnp.bfloat16),
        ],
        compiler_params=pltpu.CompilerParams(vmem_limit_bytes=24 << 20),
        name="ladder",
    )(*t_pieces, *v_pieces, residual_in, pair_rows, ab_rows)


def solution(mesh):
    placed = (P("pair", "virt"), P("virt", "pair"), P("pair", "virt"), P("pair"), P("virt"), P())
    return jax.shard_map(
        shards, mesh=mesh, in_specs=placed, out_specs=P("pair", "virt"), check_vma=False
    )
```

```python
import jax
import jax.numpy as jnp
from jax import lax
from jax.experimental import pallas as pl
from jax.experimental.pallas import tpu as pltpu
from jax.sharding import PartitionSpec as P

BLOCK = 8
LANES = 128
TILE = 256


def column(row):
    return jnp.transpose(jnp.broadcast_to(row, (LANES, LANES)))


def compact_kernel(t_ref, v_ref, pair_ref, ab_ref, cd_ref, ct_ref, cv_ref):
    def one(x_ref, irrep_ref, index, out_ref):
        held = x_ref.shape[0]
        per_row = LANES // held
        labels = column(cd_ref[pl.ds(index // per_row, 1), :])
        part = labels[:held]
        for step in range(1, per_row):
            part = jnp.where(index % per_row == step, labels[step * held : (step + 1) * held], part)
        for group in range(x_ref.shape[1] // LANES):
            lanes = slice(group * LANES, (group + 1) * LANES)
            kept = jnp.where(part == irrep_ref[group : group + 1, :], x_ref[:, lanes], 0.0)
            out_ref[:, lanes] = jnp.sum(kept.reshape(held // BLOCK, BLOCK, LANES), axis=1)

    one(t_ref, pair_ref, lax.axis_index("virt"), ct_ref)
    one(v_ref, ab_ref, lax.axis_index("pair"), cv_ref)


def split(x):
    high = x.astype(jnp.bfloat16)
    low = (x - high.astype(jnp.float32)).astype(jnp.bfloat16)
    return high, low


def stage_kernel(v_order, *refs):
    v_refs = refs[: len(v_order)]
    residual_ref, staged_ref, v_split, v_rows, sem = refs[len(v_order) :]
    copy = pltpu.make_async_copy(residual_ref, staged_ref, sem)
    copy.start()
    depth = v_rows.shape[0]
    apart = lax.axis_index("virt") ^ lax.axis_index("pair")
    for order, ref in zip(v_order, v_refs):
        for slot, k in enumerate(order):
            at = pl.multiple_of((apart ^ k) * BLOCK, BLOCK)
            v_rows[pl.ds(at, BLOCK), :] = ref[slot * BLOCK : (slot + 1) * BLOCK, :]
    high, low = split(v_rows[...])
    v_split[:depth, :] = high
    v_split[depth : 2 * depth, :] = low
    v_split[2 * depth :, :] = high
    copy.wait()


def ladder_kernel(t_order, *refs):
    t_refs = refs[: len(t_order)]
    residual_ref, v_split, pair_ref, ab_ref, out_ref, t_rows, tiles, sems = refs[len(t_order) :]
    for order, ref in zip(t_order, t_refs):
        for slot, k in enumerate(order):
            t_rows[k * BLOCK : (k + 1) * BLOCK, :] = ref[slot * BLOCK : (slot + 1) * BLOCK, :]
    copies = []
    for tile in range(residual_ref.shape[0] // TILE):
        rows = slice(tile * TILE, (tile + 1) * TILE)
        high, low = split(jnp.transpose(t_rows[:, rows]))
        products = jnp.dot(
            jnp.concatenate([high, high, low], axis=1), v_split[...], preferred_element_type=jnp.float32
        )
        for part in range(TILE // LANES):
            row = tile * (TILE // LANES) + part
            at = slice(row * LANES, (row + 1) * LANES)
            labels = column(pair_ref[row : row + 1, :])
            for group in range(residual_ref.shape[1] // LANES):
                lanes = slice(group * LANES, (group + 1) * LANES)
                same = labels == ab_ref[group : group + 1, :]
                term = products[part * LANES : (part + 1) * LANES, lanes]
                tiles[at, lanes] = residual_ref[at, lanes] + jnp.where(same, term, 0.0)
        copies.append(pltpu.make_async_copy(tiles.at[rows, :], out_ref.at[rows, :], sems.at[tile]))
        copies[-1].start()
    for copy in copies:
        copy.wait()


def pairs(k):
    return [(i, i ^ k) for i in range(16)]


def exchange(x, axis, stage):
    return [lax.ppermute(x, axis, pairs(k)) for k in stage]


def gather(x, axis, stages):
    held, order = x, [0]
    for stage in stages[:-1]:
        held = jnp.concatenate([held, *exchange(held, axis, stage)], 0)
        order = [o ^ k for k in (0, *stage) for o in order]
    pieces = [held, *exchange(held, axis, stages[-1])]
    return pieces, [tuple(o ^ k for o in order) for k in (0, *stages[-1])]


def shards(amplitudes, integrals, residual_in, pair_irrep, ab_irrep, cd_irrep):
    rows, columns = residual_in.shape
    held_t, held_v = amplitudes.shape[1], integrals.shape[1]
    pair_rows = pair_irrep.reshape(-1, LANES)
    ab_rows = ab_irrep.reshape(-1, LANES)
    own_t, own_v = pl.pallas_call(
        compact_kernel,
        out_shape=(
            pltpu.VMEM((held_t // BLOCK, rows), jnp.float32),
            pltpu.VMEM((held_v // BLOCK, columns), jnp.float32),
        ),
        name="compact",
    )(amplitudes.T, integrals.T, pair_rows, ab_rows, cd_irrep.reshape(-1, LANES))
    t_pieces, t_order = gather(own_t, "virt", ((1, 3, 2), (4, 12, 8)))
    v_pieces, v_order = gather(own_v, "pair", ((8, 4, 12), (2,), (1,)))
    depth = 16 * BLOCK
    whole = pl.BlockSpec(memory_space=pltpu.VMEM)
    anywhere = pl.BlockSpec(memory_space=pl.ANY)
    staged, v_split = pl.pallas_call(
        lambda *refs: stage_kernel(v_order, *refs),
        in_specs=[whole] * len(v_pieces) + [anywhere],
        out_specs=[whole, whole],
        out_shape=(
            pltpu.VMEM((rows, columns), jnp.float32),
            pltpu.VMEM((3 * depth, columns), jnp.bfloat16),
        ),
        scratch_shapes=[pltpu.VMEM((depth, columns), jnp.float32), pltpu.SemaphoreType.DMA(())],
        compiler_params=pltpu.CompilerParams(vmem_limit_bytes=16 << 20),
        cost_estimate=pl.CostEstimate(flops=0, transcendentals=0, bytes_accessed=8 * rows * columns),
        name="stage",
    )(*v_pieces, pltpu.with_memory_space_constraint(residual_in, pltpu.HBM))
    return pl.pallas_call(
        lambda *refs: ladder_kernel(t_order, *refs),
        in_specs=[whole] * (len(t_pieces) + 4),
        out_specs=anywhere,
        out_shape=jax.ShapeDtypeStruct((rows, columns), jnp.float32),
        scratch_shapes=[
            pltpu.VMEM((depth, rows), jnp.float32),
            pltpu.VMEM((rows, columns), jnp.float32),
            pltpu.SemaphoreType.DMA((rows // TILE,)),
        ],
        compiler_params=pltpu.CompilerParams(vmem_limit_bytes=24 << 20),
        name="ladder",
    )(*t_pieces, staged, v_split, pair_rows, ab_rows)


def solution(mesh):
    placed = (P("pair", "virt"), P("virt", "pair"), P("pair", "virt"), P("pair"), P("virt"), P())
    return jax.shard_map(
        shards, mesh=mesh, in_specs=placed, out_specs=P("pair", "virt"), check_vma=False
    )
```

```python
import jax
import jax.numpy as jnp
from jax import lax
from jax.experimental import pallas as pl
from jax.experimental.pallas import tpu as pltpu
from jax.sharding import PartitionSpec as P

BLOCK = 8
LANES = 128
TILE = 256


def column(row):
    return jnp.transpose(jnp.broadcast_to(row, (LANES, LANES)))


def compact_kernel(t_ref, v_ref, pair_ref, ab_ref, cd_ref, ct_ref, cv_ref):
    def one(x_ref, irrep_ref, index, out_ref):
        held = x_ref.shape[0]
        per_row = LANES // held
        labels = column(cd_ref[pl.ds(index // per_row, 1), :])
        part = labels[:held]
        for step in range(1, per_row):
            part = jnp.where(index % per_row == step, labels[step * held : (step + 1) * held], part)
        for group in range(x_ref.shape[1] // LANES):
            lanes = slice(group * LANES, (group + 1) * LANES)
            kept = jnp.where(part == irrep_ref[group : group + 1, :], x_ref[:, lanes], 0.0)
            out_ref[:, lanes] = jnp.sum(kept.reshape(held // BLOCK, BLOCK, LANES), axis=1)

    one(t_ref, pair_ref, lax.axis_index("virt"), ct_ref)
    one(v_ref, ab_ref, lax.axis_index("pair"), cv_ref)


def split(x):
    high = x.astype(jnp.bfloat16)
    low = (x - high.astype(jnp.float32)).astype(jnp.bfloat16)
    return high, low


def stage_kernel(residual_ref, after_ref, staged_ref, sem):
    copy = pltpu.make_async_copy(residual_ref, staged_ref, sem)
    copy.start()
    copy.wait()


def turn_kernel(t_order, *refs):
    t_refs = refs[: len(t_order)]
    t_split, t_rows = refs[len(t_order) :]
    depth = t_rows.shape[0]
    for order, ref in zip(t_order, t_refs):
        for slot, k in enumerate(order):
            t_rows[k * BLOCK : (k + 1) * BLOCK, :] = ref[slot * BLOCK : (slot + 1) * BLOCK, :]
    for group in range(t_rows.shape[1] // LANES):
        rows = slice(group * LANES, (group + 1) * LANES)
        high, low = split(jnp.transpose(t_rows[:, rows]))
        t_split[rows, :depth] = high
        t_split[rows, depth : 2 * depth] = high
        t_split[rows, 2 * depth :] = low


def ladder_kernel(v_order, *refs):
    v_refs = refs[: len(v_order)]
    residual_ref, t_split, pair_ref, ab_ref, out_ref, v_rows, v_split, tiles, sems = refs[len(v_order) :]
    depth = v_rows.shape[0]
    apart = lax.axis_index("virt") ^ lax.axis_index("pair")
    for order, ref in zip(v_order, v_refs):
        for slot, k in enumerate(order):
            at = pl.multiple_of((apart ^ k) * BLOCK, BLOCK)
            v_rows[pl.ds(at, BLOCK), :] = ref[slot * BLOCK : (slot + 1) * BLOCK, :]
    high, low = split(v_rows[...])
    v_split[:depth, :] = high
    v_split[depth : 2 * depth, :] = low
    v_split[2 * depth :, :] = high
    copies = []
    for tile in range(residual_ref.shape[0] // TILE):
        rows = slice(tile * TILE, (tile + 1) * TILE)
        products = jnp.dot(t_split[rows, :], v_split[...], preferred_element_type=jnp.float32)
        for part in range(TILE // LANES):
            row = tile * (TILE // LANES) + part
            at = slice(row * LANES, (row + 1) * LANES)
            labels = column(pair_ref[row : row + 1, :])
            for group in range(residual_ref.shape[1] // LANES):
                lanes = slice(group * LANES, (group + 1) * LANES)
                same = labels == ab_ref[group : group + 1, :]
                term = products[part * LANES : (part + 1) * LANES, lanes]
                tiles[at, lanes] = residual_ref[at, lanes] + jnp.where(same, term, 0.0)
        copies.append(pltpu.make_async_copy(tiles.at[rows, :], out_ref.at[rows, :], sems.at[tile]))
        copies[-1].start()
    for copy in copies:
        copy.wait()


bar = lax.optimization_barrier
def cat(*l): return jnp.concatenate(l, 0)
def T(x,k): return lax.ppermute(x,"virt",pairs(k))
def V(x,k): return lax.ppermute(x,"pair",pairs(k))
def orders(base, ks): return [tuple(o ^ k for o in base) for k in ks]


def pairs(k):
    return [(i, i ^ k) for i in range(16)]


def exchange(x, axis, stage):
    return [lax.ppermute(x, axis, pairs(k)) for k in stage]


def gather(x, axis, stages):
    held, order = x, [0]
    for stage in stages[:-1]:
        held = jnp.concatenate([held, *exchange(held, axis, stage)], 0)
        order = [o ^ k for k in (0, *stage) for o in order]
    pieces = [held, *exchange(held, axis, stages[-1])]
    return pieces, [tuple(o ^ k for o in order) for k in (0, *stages[-1])]


def shards(amplitudes, integrals, residual_in, pair_irrep, ab_irrep, cd_irrep):
    rows, columns = residual_in.shape
    held_t, held_v = amplitudes.shape[1], integrals.shape[1]
    pair_rows = pair_irrep.reshape(-1, LANES)
    ab_rows = ab_irrep.reshape(-1, LANES)
    own_t, own_v = pl.pallas_call(
        compact_kernel,
        out_shape=(
            pltpu.VMEM((held_t // BLOCK, rows), jnp.float32),
            pltpu.VMEM((held_v // BLOCK, columns), jnp.float32),
        ),
        name="compact",
    )(amplitudes.T, integrals.T, pair_rows, ab_rows, cd_irrep.reshape(-1, LANES))
    t1 = cat(own_t, T(own_t,1)); ZO=(0,1,3,2)
    v1 = cat(own_v, V(own_v,4)); VO1=(0,4)
    tz = cat(t1, T(t1,3))
    v2 = cat(v1, V(v1,12)); VO2=tuple(o ^ k for k in (0,12) for o in VO1)
    tx = cat(tz, T(tz,4))
    t_pieces, t_order = [tx, T(tx,12)], orders(tuple(o ^ k for k in (0,4) for o in ZO), (0,12))
    v3 = cat(v2, V(v2,2))
    v_pieces, v_order = [v3, V(v3,1)], orders(tuple(o ^ k for k in (0,2) for o in VO2), (0,1))
    depth = 16 * BLOCK
    whole = pl.BlockSpec(memory_space=pltpu.VMEM)
    anywhere = pl.BlockSpec(memory_space=pl.ANY)
    staged = pl.pallas_call(
        stage_kernel,
        in_specs=[anywhere, anywhere],
        out_specs=whole,
        out_shape=pltpu.VMEM((rows, columns), jnp.float32),
        scratch_shapes=[pltpu.SemaphoreType.DMA(())],
        cost_estimate=pl.CostEstimate(flops=0, transcendentals=0, bytes_accessed=8388608),
        compiler_params=pltpu.CompilerParams(vmem_limit_bytes=2 << 20),
        name="stage",
    )(pltpu.with_memory_space_constraint(residual_in, pltpu.HBM), t_pieces[0])
    t_split = pl.pallas_call(
        lambda *refs: turn_kernel(t_order, *refs),
        in_specs=[whole] * len(t_pieces),
        out_specs=whole,
        out_shape=pltpu.VMEM((rows, 3 * depth), jnp.bfloat16),
        scratch_shapes=[pltpu.VMEM((depth, rows), jnp.float32)],
        cost_estimate=pl.CostEstimate(flops=0, transcendentals=0, bytes_accessed=8388608),
        compiler_params=pltpu.CompilerParams(vmem_limit_bytes=8 << 20),
        name="turn",
    )(*t_pieces)
    return pl.pallas_call(
        lambda *refs: ladder_kernel(v_order, *refs),
        in_specs=[whole] * (len(v_pieces) + 4),
        out_specs=anywhere,
        out_shape=jax.ShapeDtypeStruct((rows, columns), jnp.float32),
        scratch_shapes=[
            pltpu.VMEM((depth, columns), jnp.float32),
            pltpu.VMEM((3 * depth, columns), jnp.bfloat16),
            pltpu.VMEM((rows, columns), jnp.float32),
            pltpu.SemaphoreType.DMA((rows // TILE,)),
        ],
        compiler_params=pltpu.CompilerParams(vmem_limit_bytes=24 << 20),
        name="ladder",
    )(*v_pieces, staged, t_split, pair_rows, ab_rows)


def solution(mesh):
    placed = (P("pair", "virt"), P("virt", "pair"), P("pair", "virt"), P("pair"), P("virt"), P())
    return jax.shard_map(
        shards, mesh=mesh, in_specs=placed, out_specs=P("pair", "virt"), check_vma=False
    )
```

```python
import jax
import jax.numpy as jnp
from jax import lax
from jax.experimental import pallas as pl
from jax.experimental.pallas import tpu as pltpu
from jax.sharding import PartitionSpec as P

BLOCK = 8
LANES = 128
TILE = 128


def column(row):
    return jnp.transpose(jnp.broadcast_to(row, (LANES, LANES)))


def compact_kernel(axis, x_ref, irrep_ref, cd_ref, out_ref):
    index = lax.axis_index(axis)
    held = x_ref.shape[0]
    per_row = LANES // held
    labels = column(cd_ref[pl.ds(index // per_row, 1), :])
    part = labels[:held]
    for step in range(1, per_row):
        part = jnp.where(index % per_row == step, labels[step * held : (step + 1) * held], part)
    for group in range(x_ref.shape[1] // LANES):
        lanes = slice(group * LANES, (group + 1) * LANES)
        kept = jnp.where(part == irrep_ref[group : group + 1, :], x_ref[:, lanes], 0.0)
        out_ref[:, lanes] = jnp.sum(kept.reshape(held // BLOCK, BLOCK, LANES), axis=1)


def compact(x, irrep_rows, cd_rows, axis):
    return pl.pallas_call(
        lambda *refs: compact_kernel(axis, *refs),
        out_shape=pltpu.VMEM((x.shape[1] // BLOCK, x.shape[0]), jnp.float32),
        cost_estimate=pl.CostEstimate(flops=0, transcendentals=0, bytes_accessed=1048576),
        compiler_params=pltpu.CompilerParams(vmem_limit_bytes=4 << 20),
        name="compact_" + axis,
    )(*(pltpu.with_memory_space_constraint(a, pltpu.HBM) for a in (x.T, irrep_rows, cd_rows)))


def split(x):
    high = x.astype(jnp.bfloat16)
    low = (x - high.astype(jnp.float32)).astype(jnp.bfloat16)
    return high, low


def stage_kernel(residual_ref, after_ref, staged_ref, sem):
    copy = pltpu.make_async_copy(residual_ref, staged_ref, sem)
    copy.start()
    copy.wait()


def turn_kernel(t_order, *refs):
    t_refs = refs[: len(t_order)]
    t_split, t_rows = refs[len(t_order) :]
    depth = t_rows.shape[0]
    for order, ref in zip(t_order, t_refs):
        for slot, k in enumerate(order):
            t_rows[k * BLOCK : (k + 1) * BLOCK, :] = ref[slot * BLOCK : (slot + 1) * BLOCK, :]
    for group in range(t_rows.shape[1] // LANES):
        rows = slice(group * LANES, (group + 1) * LANES)
        high, low = split(jnp.transpose(t_rows[:, rows]))
        t_split[rows, :depth] = high
        t_split[rows, depth : 2 * depth] = high
        t_split[rows, 2 * depth :] = low


def ladder_kernel(v_order, *refs):
    v_refs = refs[: len(v_order)]
    residual_ref, t_split, pair_ref, ab_ref, out_ref, v_rows, v_split, tiles, sems = refs[len(v_order) :]
    depth = v_rows.shape[0]
    apart = lax.axis_index("virt") ^ lax.axis_index("pair")
    for order, ref in zip(v_order, v_refs):
        for slot, k in enumerate(order):
            at = pl.multiple_of((apart ^ k) * BLOCK, BLOCK)
            v_rows[pl.ds(at, BLOCK), :] = ref[slot * BLOCK : (slot + 1) * BLOCK, :]
    high, low = split(v_rows[...])
    v_split[:depth, :] = high
    v_split[depth : 2 * depth, :] = low
    v_split[2 * depth :, :] = high
    copies = []
    for tile in range(residual_ref.shape[0] // TILE):
        rows = slice(tile * TILE, (tile + 1) * TILE)
        products = jnp.dot(t_split[rows, :], v_split[...], preferred_element_type=jnp.float32)
        for part in range(TILE // LANES):
            row = tile * (TILE // LANES) + part
            at = slice(row * LANES, (row + 1) * LANES)
            labels = column(pair_ref[row : row + 1, :])
            for group in range(residual_ref.shape[1] // LANES):
                lanes = slice(group * LANES, (group + 1) * LANES)
                same = labels == ab_ref[group : group + 1, :]
                term = products[part * LANES : (part + 1) * LANES, lanes]
                tiles[at, lanes] = residual_ref[at, lanes] + jnp.where(same, term, 0.0)
        copies.append(pltpu.make_async_copy(tiles.at[rows, :], out_ref.at[rows, :], sems.at[tile]))
        copies[-1].start()
    for copy in copies:
        copy.wait()


bar = lax.optimization_barrier
def cat(*l): return jnp.concatenate(l, 0)
def T(x,k): return lax.ppermute(x,"virt",pairs(k))
def V(x,k): return lax.ppermute(x,"pair",pairs(k))
def orders(base, ks): return [tuple(o ^ k for o in base) for k in ks]


def pairs(k):
    return [(i, i ^ k) for i in range(16)]


def exchange(x, axis, stage):
    return [lax.ppermute(x, axis, pairs(k)) for k in stage]


def gather(x, axis, stages):
    held, order = x, [0]
    for stage in stages[:-1]:
        held = jnp.concatenate([held, *exchange(held, axis, stage)], 0)
        order = [o ^ k for k in (0, *stage) for o in order]
    pieces = [held, *exchange(held, axis, stages[-1])]
    return pieces, [tuple(o ^ k for o in order) for k in (0, *stages[-1])]


def shards(amplitudes, integrals, residual_in, pair_irrep, ab_irrep, cd_irrep):
    rows, columns = residual_in.shape
    pair_rows = pair_irrep.reshape(-1, LANES)
    ab_rows = ab_irrep.reshape(-1, LANES)
    cd_rows = cd_irrep.reshape(-1, LANES)
    own_t = compact(amplitudes, pair_rows, cd_rows, "virt")
    own_v = compact(integrals, ab_rows, cd_rows, "pair")
    t1 = cat(own_t, T(own_t,1)); ZO=(0,1,3,2)
    v1 = cat(own_v, V(own_v,2)); VO1=(0,2)
    tz = cat(t1, T(t1,3))
    v2 = cat(v1, V(v1,4)); VO2=tuple(o ^ k for k in (0,4) for o in VO1)
    tx = cat(tz, T(tz,4))
    t_pieces, t_order = [tx, T(tx,12)], orders(tuple(o ^ k for k in (0,4) for o in ZO), (0,12))
    v3 = cat(v2, V(v2,12))
    v_pieces, v_order = [v3, V(v3,1)], orders(tuple(o ^ k for k in (0,12) for o in VO2), (0,1))
    depth = 16 * BLOCK
    whole = pl.BlockSpec(memory_space=pltpu.VMEM)
    anywhere = pl.BlockSpec(memory_space=pl.ANY)
    staged = pl.pallas_call(
        stage_kernel,
        in_specs=[anywhere, anywhere],
        out_specs=whole,
        out_shape=pltpu.VMEM((rows, columns), jnp.float32),
        scratch_shapes=[pltpu.SemaphoreType.DMA(())],
        cost_estimate=pl.CostEstimate(flops=0, transcendentals=0, bytes_accessed=8388608),
        compiler_params=pltpu.CompilerParams(vmem_limit_bytes=2 << 20),
        name="stage",
    )(pltpu.with_memory_space_constraint(residual_in, pltpu.HBM), t_pieces[0])
    t_split = pl.pallas_call(
        lambda *refs: turn_kernel(t_order, *refs),
        in_specs=[whole] * len(t_pieces),
        out_specs=whole,
        out_shape=pltpu.VMEM((rows, 3 * depth), jnp.bfloat16),
        scratch_shapes=[pltpu.VMEM((depth, rows), jnp.float32)],
        cost_estimate=pl.CostEstimate(flops=0, transcendentals=0, bytes_accessed=8388608),
        compiler_params=pltpu.CompilerParams(vmem_limit_bytes=8 << 20),
        name="turn",
    )(*t_pieces)
    return pl.pallas_call(
        lambda *refs: ladder_kernel(v_order, *refs),
        in_specs=[whole] * (len(v_pieces) + 4),
        out_specs=anywhere,
        out_shape=jax.ShapeDtypeStruct((rows, columns), jnp.float32),
        scratch_shapes=[
            pltpu.VMEM((depth, columns), jnp.float32),
            pltpu.VMEM((3 * depth, columns), jnp.bfloat16),
            pltpu.VMEM((rows, columns), jnp.float32),
            pltpu.SemaphoreType.DMA((rows // TILE,)),
        ],
        compiler_params=pltpu.CompilerParams(vmem_limit_bytes=24 << 20),
        name="ladder",
    )(*v_pieces, staged, t_split, pair_rows, ab_rows)


def solution(mesh):
    placed = (P("pair", "virt"), P("virt", "pair"), P("pair", "virt"), P("pair"), P("virt"), P())
    return jax.shard_map(
        shards, mesh=mesh, in_specs=placed, out_specs=P("pair", "virt"), check_vma=False
    )
```

```python
import jax
import jax.numpy as jnp
from jax import lax
from jax.experimental import pallas as pl
from jax.experimental.pallas import tpu as pltpu
from jax.sharding import PartitionSpec as P

BLOCK = 8
LANES = 128
TILE = 128


def column(row):
    return jnp.transpose(jnp.broadcast_to(row, (LANES, LANES)))


def compact_kernel(axis, x_ref, irrep_ref, cd_ref, out_ref):
    index = lax.axis_index(axis)
    held = x_ref.shape[0]
    per_row = LANES // held
    labels = column(cd_ref[pl.ds(index // per_row, 1), :])
    part = labels[:held]
    for step in range(1, per_row):
        part = jnp.where(index % per_row == step, labels[step * held : (step + 1) * held], part)
    for group in range(x_ref.shape[1] // LANES):
        lanes = slice(group * LANES, (group + 1) * LANES)
        kept = jnp.where(part == irrep_ref[group : group + 1, :], x_ref[:, lanes], 0.0)
        out_ref[:, lanes] = jnp.sum(kept.reshape(held // BLOCK, BLOCK, LANES), axis=1)


def compact(x, irrep_rows, cd_rows, axis):
    return pl.pallas_call(
        lambda *refs: compact_kernel(axis, *refs),
        out_shape=pltpu.VMEM((x.shape[1] // BLOCK, x.shape[0]), jnp.float32),
        cost_estimate=pl.CostEstimate(flops=0, transcendentals=0, bytes_accessed=1048576),
        compiler_params=pltpu.CompilerParams(vmem_limit_bytes=4 << 20),
        name="compact_" + axis,
    )(*(pltpu.with_memory_space_constraint(a, pltpu.HBM) for a in (x.T, irrep_rows, cd_rows)))


def split(x):
    high = x.astype(jnp.bfloat16)
    low = (x - high.astype(jnp.float32)).astype(jnp.bfloat16)
    return high, low


def stage_kernel(residual_ref, after_ref, staged_ref, sem):
    copy = pltpu.make_async_copy(residual_ref, staged_ref, sem)
    copy.start()
    copy.wait()


def turn_kernel(t_order, *refs):
    t_refs = refs[: len(t_order)]
    t_split, t_rows = refs[len(t_order) :]
    depth = t_rows.shape[0]
    for order, ref in zip(t_order, t_refs):
        for slot, k in enumerate(order):
            t_rows[k * BLOCK : (k + 1) * BLOCK, :] = ref[slot * BLOCK : (slot + 1) * BLOCK, :]
    for group in range(t_rows.shape[1] // LANES):
        rows = slice(group * LANES, (group + 1) * LANES)
        high, low = split(jnp.transpose(t_rows[:, rows]))
        t_split[rows, :depth] = high
        t_split[rows, depth : 2 * depth] = high
        t_split[rows, 2 * depth :] = low


def lay_kernel(v_order, *refs):
    v_refs = refs[: len(v_order)]
    v_split, v_rows = refs[len(v_order) :]
    depth = v_rows.shape[0]
    apart = lax.axis_index("virt") ^ lax.axis_index("pair")
    for order, ref in zip(v_order, v_refs):
        for slot, k in enumerate(order):
            at = pl.multiple_of((apart ^ k) * BLOCK, BLOCK)
            v_rows[pl.ds(at, BLOCK), :] = ref[slot * BLOCK : (slot + 1) * BLOCK, :]
    high, low = split(v_rows[...])
    v_split[:depth, :] = high
    v_split[depth : 2 * depth, :] = low
    v_split[2 * depth :, :] = high


def ladder_kernel(residual_ref, t_split, v_split, pair_ref, ab_ref, out_ref, tiles, sems):
    copies = []
    for tile in range(residual_ref.shape[0] // TILE):
        rows = slice(tile * TILE, (tile + 1) * TILE)
        products = jnp.dot(t_split[rows, :], v_split[...], preferred_element_type=jnp.float32)
        for part in range(TILE // LANES):
            row = tile * (TILE // LANES) + part
            at = slice(row * LANES, (row + 1) * LANES)
            labels = column(pair_ref[row : row + 1, :])
            for group in range(residual_ref.shape[1] // LANES):
                lanes = slice(group * LANES, (group + 1) * LANES)
                same = labels == ab_ref[group : group + 1, :]
                term = products[part * LANES : (part + 1) * LANES, lanes]
                tiles[at, lanes] = residual_ref[at, lanes] + jnp.where(same, term, 0.0)
        copies.append(pltpu.make_async_copy(tiles.at[rows, :], out_ref.at[rows, :], sems.at[tile]))
        copies[-1].start()
    for copy in copies:
        copy.wait()


bar = lax.optimization_barrier
def cat(*l): return jnp.concatenate(l, 0)
def T(x,k): return lax.ppermute(x,"virt",pairs(k))
def V(x,k): return lax.ppermute(x,"pair",pairs(k))
def orders(base, ks): return [tuple(o ^ k for o in base) for k in ks]


def pairs(k):
    return [(i, i ^ k) for i in range(16)]


def exchange(x, axis, stage):
    return [lax.ppermute(x, axis, pairs(k)) for k in stage]


def gather(x, axis, stages):
    held, order = x, [0]
    for stage in stages[:-1]:
        held = jnp.concatenate([held, *exchange(held, axis, stage)], 0)
        order = [o ^ k for k in (0, *stage) for o in order]
    pieces = [held, *exchange(held, axis, stages[-1])]
    return pieces, [tuple(o ^ k for o in order) for k in (0, *stages[-1])]


def shards(amplitudes, integrals, residual_in, pair_irrep, ab_irrep, cd_irrep):
    rows, columns = residual_in.shape
    pair_rows = pair_irrep.reshape(-1, LANES)
    ab_rows = ab_irrep.reshape(-1, LANES)
    cd_rows = cd_irrep.reshape(-1, LANES)
    own_t = compact(amplitudes, pair_rows, cd_rows, "virt")
    own_v = compact(integrals, ab_rows, cd_rows, "pair")
    t1 = cat(own_t, T(own_t,1)); ZO=(0,1,3,2)
    v1 = cat(own_v, V(own_v,2)); VO1=(0,2)
    tz = cat(t1, T(t1,3))
    v2 = cat(v1, V(v1,4)); VO2=tuple(o ^ k for k in (0,4) for o in VO1)
    tx = cat(tz, T(tz,4))
    t_pieces, t_order = [tx, T(tx,12)], orders(tuple(o ^ k for k in (0,4) for o in ZO), (0,12))
    v3 = cat(v2, V(v2,12))
    v_pieces, v_order = [v3, V(v3,1)], orders(tuple(o ^ k for k in (0,12) for o in VO2), (0,1))
    depth = 16 * BLOCK
    whole = pl.BlockSpec(memory_space=pltpu.VMEM)
    anywhere = pl.BlockSpec(memory_space=pl.ANY)
    staged = pl.pallas_call(
        stage_kernel,
        in_specs=[anywhere, anywhere],
        out_specs=whole,
        out_shape=pltpu.VMEM((rows, columns), jnp.float32),
        scratch_shapes=[pltpu.SemaphoreType.DMA(())],
        cost_estimate=pl.CostEstimate(flops=0, transcendentals=0, bytes_accessed=8388608),
        compiler_params=pltpu.CompilerParams(vmem_limit_bytes=2 << 20),
        name="stage",
    )(pltpu.with_memory_space_constraint(residual_in, pltpu.HBM), t_pieces[0])
    t_split = pl.pallas_call(
        lambda *refs: turn_kernel(t_order, *refs),
        in_specs=[whole] * len(t_pieces),
        out_specs=whole,
        out_shape=pltpu.VMEM((rows, 3 * depth), jnp.bfloat16),
        scratch_shapes=[pltpu.VMEM((depth, rows), jnp.float32)],
        cost_estimate=pl.CostEstimate(flops=0, transcendentals=0, bytes_accessed=8388608),
        compiler_params=pltpu.CompilerParams(vmem_limit_bytes=8 << 20),
        name="turn",
    )(*t_pieces)
    v_split = pl.pallas_call(
        lambda *refs: lay_kernel(v_order, *refs),
        in_specs=[whole] * len(v_pieces),
        out_specs=whole,
        out_shape=pltpu.VMEM((3 * depth, columns), jnp.bfloat16),
        scratch_shapes=[pltpu.VMEM((depth, columns), jnp.float32)],
        cost_estimate=pl.CostEstimate(flops=0, transcendentals=0, bytes_accessed=0),
        compiler_params=pltpu.CompilerParams(vmem_limit_bytes=4 << 20),
        name="lay",
    )(*v_pieces)
    return pl.pallas_call(
        ladder_kernel,
        in_specs=[whole] * 5,
        out_specs=anywhere,
        out_shape=jax.ShapeDtypeStruct((rows, columns), jnp.float32),
        scratch_shapes=[
            pltpu.VMEM((rows, columns), jnp.float32),
            pltpu.SemaphoreType.DMA((rows // TILE,)),
        ],
        compiler_params=pltpu.CompilerParams(vmem_limit_bytes=24 << 20),
        name="ladder",
    )(staged, t_split, v_split, pair_rows, ab_rows)


def solution(mesh):
    placed = (P("pair", "virt"), P("virt", "pair"), P("pair", "virt"), P("pair"), P("virt"), P())
    return jax.shard_map(
        shards, mesh=mesh, in_specs=placed, out_specs=P("pair", "virt"), check_vma=False
    )
```
